32 devices in a mesh: gz: 8 (over z, x), gy: 4 (over y, core).
Axes of the slice: x: 2, y: 2, z: 4, core: 2. Of those that a mesh axis runs over, the one named last changes fastest.
Arguments:
- parcel_cell: int32 [131072], P(('gz', 'gy')), may hold values from 0 to 131071
- parcel_offset: float32 [3, 131072], P(None, ('gz', 'gy')), may hold values from 0 to 1
- parcel_volume: float32 [131072], P(('gz', 'gy')), may hold values from 1 to 8
- parcel_force: float32 [3, 131072], P(None, ('gz', 'gy')), may hold values from -24 to 24
- brick_counts: int32 [8, 4], P('gz', 'gy'), may hold values from 1 to 4096, as said below
- divergence: float32 [64, 256, 256], P('gz', 'gy'), may hold values from -6 to 6
- pressure_prev: float32 [64, 256, 256], P('gz', 'gy'), may hold values from -6 to 6
- gas_density: float32 [64, 256, 256], P('gz', 'gy'), may hold values from 0.5 to 2
Outputs:
- gas_fraction: float32 [64, 256, 256], P('gz', 'gy')
- momentum_source: float32 [64, 3, 256, 256], P('gz', None, 'gy')
- pressure: float32 [64, 256, 256], P('gz', 'gy')
- residual: float32 [64, 256, 256], P('gz', 'gy')
The draws below stay inside these ranges and needn't reach their ends.
Inputs may be any that keep to these rules, and one draw needn't show every extreme that they name: brick_counts gives the number of live parcels of each brick, held in the brick's first slots; one brick holds exactly 4096 and one exactly 1.
All inputs are finite; a program needn't handle non-finite values.
Results may differ from the reference program's by a relative error of at most 0.0021.
Values sent between devices are 32-bit elements; how exact they have to be, the bound alone decides.
A program may use at most 64 MiB of HBM per device.

```python
import math
import jax
import jax.numpy as jnp
from jax import lax

CZ = 8
CY = 64
CX = 256
PCAP = 4096
SWEEPS = 3
ITERS = 2
BRICKS_Z = 8
BRICKS_Y = 4
NZ = 64
NY = 256
NX = 256
PARCELS = 131072


def draw_brick_counts(key, part):
    key_level = jax.random.fold_in(key, 11)
    key_jitter = jax.random.fold_in(key, 12)
    key_ranking = jax.random.fold_in(key, 13)
    bricks = BRICKS_Z * BRICKS_Y
    levels = jax.random.randint(key_level, (bricks,), 0, 4)
    jitter = jax.random.randint(key_jitter, (bricks,), 0, 64)
    counts = jnp.maximum(PCAP // jnp.left_shift(1, levels) - jitter, 1)
    ranking = jax.random.permutation(key_ranking, bricks)
    counts = counts.at[ranking[0]].set(PCAP)
    counts = counts.at[ranking[1]].set(1)
    return counts.reshape(BRICKS_Z, BRICKS_Y).astype(jnp.int32)


def plant(values, stream_key, least, high):
    shape = values.shape
    spot = [jax.random.randint(jax.random.fold_in(stream_key, axis), (), 0, shape[axis]) for axis in range(len(shape))]
    values = values.at[tuple(spot)].set(least)
    longest = shape.index(max(shape))
    spot[longest] = (spot[longest] + 1) % shape[longest]
    return values.at[tuple(spot)].set(high)


def steps_of(rng, dims, pieces, low, largest):
    factor_of, own = 1.0, jax.random.fold_in(rng, 6)
    for dim, shards_of in pieces:
        draws = jnp.exp(jax.random.uniform(jax.random.fold_in(own, dim), (shards_of,), jnp.float32, low / len(pieces), largest / len(pieces)))
        factor_of = factor_of * jnp.repeat(draws, dims[dim] // shards_of).reshape([-1 if axis == dim else 1 for axis in range(len(dims))])
    return factor_of


def noise(stream_key, extent, deviation, limit, split=(), kind=jnp.bfloat16):
    values = jax.random.normal(stream_key, extent, jnp.float32) * deviation
    if len(split) > 0:
        values = steps_of(stream_key, extent, split, -0.22, 0.18) * values
    return jnp.clip(values, min=-limit, max=limit).astype(kind)


def setup_inputs(seed: int = 0) -> dict:
    key_list = jax.random.split(jax.random.key(seed), 9)
    parcel_cell = plant(jax.random.randint(key_list[0], (PARCELS,), 0, CZ * CY * CX), jax.random.fold_in(key_list[0], 1), 0, (CZ * CY * CX) - 1).astype(jnp.int32)
    parcel_offset = jnp.clip(1.0 * jax.random.uniform(key_list[1], (3, PARCELS), jnp.float32) ** steps_of(key_list[1], (3, PARCELS), ((1, 32),), -0.2, 0.2), 0.0, 1.0)
    parcel_volume = jnp.clip(jnp.exp(math.log(8.0) - 2.0794415 * jax.random.uniform(key_list[2], (PARCELS,), jnp.float32) ** steps_of(key_list[2], (PARCELS,), ((0, 32),), -0.2, 0.2)), 1.0, 8.0)
    parcel_force = noise(key_list[3], (3, PARCELS), 4.0, 24.0, ((1, 32),), jnp.float32)
    brick_counts = draw_brick_counts(jax.random.fold_in(key_list[8], 71), 0)
    divergence = noise(key_list[5], (NZ, NY, NX), 1.0, 6.0, ((0, 8), (1, 4)), jnp.float32)
    pressure_prev = noise(key_list[6], (NZ, NY, NX), 1.0, 6.0, ((0, 8), (1, 4)), jnp.float32)
    gas_density = jnp.clip(jnp.exp(math.log(2.0) - 1.3862944 * jax.random.uniform(key_list[7], (NZ, NY, NX), jnp.float32) ** steps_of(key_list[7], (NZ, NY, NX), ((0, 8), (1, 4)), -0.2, 0.2)), 0.5, 2.0)
    return dict(parcel_cell=parcel_cell, parcel_offset=parcel_offset, parcel_volume=parcel_volume, parcel_force=parcel_force, brick_counts=brick_counts, divergence=divergence, pressure_prev=pressure_prev, gas_density=gas_density)


smooth_rate = 0.15
stiffness = 0.002


def tap_weight(distance):
    return jnp.exp(-0.5 * distance * distance)


def tap_norm(offset, home_cell, upper_bound):
    summed = jnp.zeros_like(offset)
    for shift_tap in range(-3, 4):
        inside = (home_cell + shift_tap >= 0) & (home_cell + shift_tap < upper_bound)
        summed = summed + jnp.where(inside, tap_weight(shift_tap + 0.5 - offset), 0.0)
    return summed


def axis_weights(home_cell, offset, upper_bound, norm_value):
    tap_list = jnp.arange(-3, 4, dtype=jnp.int32)
    places = home_cell[:, None] + tap_list[None, :]
    distance = tap_list[None, :].astype(jnp.float32) + 0.5 - offset[:, None]
    inside = (places >= 0) & (places < upper_bound)
    weights = jnp.where(inside, tap_weight(distance), 0.0) / norm_value[:, None]
    return weights, jnp.clip(places, 0, upper_bound - 1)


def smooth_field(values):
    size_y, size_x = values.shape[1], values.shape[2]
    padded = jnp.pad(values, ((0, 0), (1, 1), (1, 1)))
    beside = jnp.roll(values, 1, 0) + jnp.roll(values, -1, 0) + padded[:, :-2, 1:-1] + padded[:, 2:, 1:-1] + padded[:, 1:-1, :-2] + padded[:, 1:-1, 2:]
    rows_at = jnp.arange(size_y, dtype=jnp.int32)
    columns = jnp.arange(size_x, dtype=jnp.int32)
    count_y = (rows_at >= 1).astype(jnp.float32) + (rows_at <= size_y - 2).astype(jnp.float32)
    count_x = (columns >= 1).astype(jnp.float32) + (columns <= size_x - 2).astype(jnp.float32)
    neighbour_count = 2.0 + count_y[:, None] + count_x[None, :]
    return values + smooth_rate * (beside - neighbour_count * values)


def neighbour_list(values):
    padded = jnp.pad(values, ((0, 0), (1, 1), (1, 1)))
    return (jnp.roll(values, 1, 0), jnp.roll(values, -1, 0), padded[:, :-2, 1:-1], padded[:, 2:, 1:-1], padded[:, 1:-1, :-2], padded[:, 1:-1, 2:])


def reference(parcel_cell, parcel_offset, parcel_volume, parcel_force, brick_counts, divergence, pressure_prev, gas_density):
    slot_ids = jnp.arange(PARCELS, dtype=jnp.int32)
    brick_ids = slot_ids // PCAP
    live_slots = ((slot_ids - brick_ids * PCAP) < brick_counts.reshape(-1)[brick_ids]).astype(jnp.float32)
    parcel_load = jnp.concatenate([parcel_volume[None, :], parcel_volume[None, :] * parcel_force], axis=0) * live_slots[None, :]
    home_z = (brick_ids // BRICKS_Y) * CZ + parcel_cell // (CY * CX)
    home_y = (brick_ids % BRICKS_Y) * CY + (parcel_cell // CX) % CY
    home_x = parcel_cell % CX
    tap_list = jnp.arange(-3, 4, dtype=jnp.int32)
    norm_z = tap_norm(parcel_offset[0], home_z * 0 + 3, 7)
    distance_z = tap_list[None, :].astype(jnp.float32) + 0.5 - parcel_offset[0][:, None]
    weight_z = tap_weight(distance_z) / norm_z[:, None]
    place_z = (home_z[:, None] + tap_list[None, :]) % NZ
    weight_y, place_y = axis_weights(home_y, parcel_offset[1], NY, tap_norm(parcel_offset[1], home_y, NY))
    weight_x, place_x = axis_weights(home_x, parcel_offset[2], NX, tap_norm(parcel_offset[2], home_x, NX))
    x_weight = lax.optimization_barrier(weight_x.astype(jnp.bfloat16)).astype(jnp.float32)
    component_ids = jnp.arange(4, dtype=jnp.int32)

    def add_plane(deposited, plane_data):
        plane_weight, plane_place = plane_data
        split_weight = (parcel_load * plane_weight[None, :])[:, :, None] * weight_y[None, :, :]
        split_weight = lax.optimization_barrier(split_weight.astype(jnp.bfloat16)).astype(jnp.float32)
        values = split_weight[:, :, :, None] * x_weight[None, :, None, :]
        deposited = deposited.at[plane_place[None, :, None, None], component_ids[:, None, None, None], place_y[None, :, :, None], place_x[None, :, None, :]].add(values)
        return deposited, None

    deposited = jnp.zeros((NZ, 4, NY, NX), jnp.float32)
    deposited, unused_out = lax.scan(add_plane, deposited, (weight_z.T, place_z.T))
    filtered = []
    for component in range(4):
        smoothed = deposited[:, component]
        for sweep_index in range(SWEEPS):
            smoothed = smooth_field(smoothed)
        filtered.append(smoothed)
    gas_fraction = 1.0 / (1.0 + filtered[0])
    momentum_source = jnp.stack(filtered[1:], axis=1)
    mobility = gas_fraction / gas_density
    face_list = [0.5 * (mobility + other) for other in neighbour_list(mobility)]
    diagonal = stiffness * mobility + face_list[0] + face_list[1] + face_list[2] + face_list[3] + face_list[4] + face_list[5]
    along_z = neighbour_list(filtered[1])
    along_y = neighbour_list(filtered[2])
    along_x = neighbour_list(filtered[3])
    spread = 0.5 * (along_z[1] - along_z[0]) + 0.5 * (along_y[3] - along_y[2]) + 0.5 * (along_x[5] - along_x[4])
    right_side = divergence - spread

    def operate(values):
        others = neighbour_list(values)
        coupled = face_list[0] * others[0] + face_list[1] * others[1] + face_list[2] * others[2] + face_list[3] * others[3] + face_list[4] * others[4] + face_list[5] * others[5]
        return diagonal * values - coupled

    pressure = pressure_prev
    residual = right_side - operate(pressure)
    precond = residual / diagonal
    direction = precond
    scaled_norm = jnp.sum(residual * precond)
    for iteration in range(ITERS):
        mapped = operate(direction)
        step_size = scaled_norm / jnp.sum(direction * mapped)
        pressure = pressure + step_size * direction
        residual = residual - step_size * mapped
        if iteration + 1 < ITERS:
            precond = residual / diagonal
            norm_next = jnp.sum(residual * precond)
            direction = precond + (norm_next / scaled_norm) * direction
            scaled_norm = norm_next
    return (gas_fraction, momentum_source, pressure, residual)
```

```python
import functools
import math

import jax
import jax.numpy as jnp
from jax import lax
from jax.experimental import pallas as pl
from jax.experimental.pallas import tpu as pltpu
from jax.sharding import PartitionSpec as P

SWEEPS = 3
REACH = 3
HALO = SWEEPS + 1
EDGE = 2 * HALO
CHUNK = 1024
LANES = 128
smooth_rate = 0.15
stiffness = 0.002
F32 = jnp.float32
MESH = pl.DeviceIdType.MESH


def tap(distance):
    return jnp.exp2((-0.5 * math.log2(math.e)) * (distance * distance))


def split_cell(cell, ny, nx):
    if ny & (ny - 1) == 0 and nx & (nx - 1) == 0:
        sx, sy = nx.bit_length() - 1, ny.bit_length() - 1
        return (
            lax.shift_right_logical(cell, sx + sy),
            lax.shift_right_logical(cell, sx) & (ny - 1),
            cell & (nx - 1),
        )
    row = lax.div(cell, nx)
    return lax.div(row, ny), lax.rem(row, ny), lax.rem(cell, nx)


def step_kernel(
    ngz, ngy, nz, ny, nx, slots,
    count_ref, cell_hbm, off_hbm, vol_hbm, force_hbm, div_hbm, p_hbm, den_hbm,
    gf_ref, mom_ref, out_ref, res_ref,
    cell_ref, off_ref, vol_ref, force_ref, div_ref, p_ref, den_ref, pk_ref, near, wz_ref, wy_ref, wx_ref, dep, fld, tile_in,
    halo_z, halo_y, edge, edge_in, mob, face_z, face_s, face_n, face_w, face_e, diag,
    r_ref, z_ref, q_ref, w_ref, aw_ref, row_ref, red,
    load_sem, near_send, near_recv, tile_send, tile_recv, hz_send, hz_recv, hy_send, hy_recv,
    row_send, row_recv,
):
    gz, gy = lax.axis_index("gz"), lax.axis_index("gy")
    planes, rows = nz + 2 * HALO, ny + EDGE
    total_y = ngy * ny
    first = gy * ny
    count = ngz * ngy
    me = gz * ngy + gy
    odd = lax.rem(gz, 2)
    up, down = lax.rem(gz + 1, ngz), lax.rem(gz + ngz - 1, ngz)
    partner, other = jnp.where(odd == 1, down, up), jnp.where(odd == 1, up, down)
    north_gy, south_gy = lax.rem(gy + 1, ngy), lax.rem(gy + ngy - 1, ngy)
    has_s, has_n = gy > 0, gy < ngy - 1

    loads = [
        pltpu.make_async_copy(src, dst, load_sem.at[n])
        for n, (src, dst) in enumerate((
            (cell_hbm, cell_ref), (off_hbm, off_ref), (vol_hbm, vol_ref), (force_hbm, force_ref),
            (den_hbm, den_ref), (p_hbm, p_ref), (div_hbm, div_ref),
        ))
    ]
    for c in loads:
        c.start()

    def place_of(d):
        to = lax.rem(me + d, count)
        to_z = lax.div(to, ngy)
        return {"gz": to_z, "gy": to - to_z * ngy}

    def each_other(body):
        if count <= 64:
            for d in range(1, count):
                body(d)
        else:
            lax.fori_loop(1, count, lambda d, carry: (body(d), carry)[1], 0)

    barrier = pltpu.get_barrier_semaphore()
    each_other(lambda d: pl.semaphore_signal(barrier, inc=1, device_id=place_of(d), device_id_type=MESH))

    for c in loads[:4]:
        c.wait()
    live = lax.broadcasted_iota(jnp.int32, (1, slots), 1) < count_ref[0, 0]
    volume = jnp.where(live, vol_ref[...], 0.0)
    pk_ref[0:1] = volume
    pk_ref[1:4] = volume * force_ref[...]
    pk_ref[4:5] = cell_ref[...].astype(F32)
    pk_ref[5:8] = off_ref[...]

    def remote(src, dst, send, recv, where):
        return pltpu.make_async_remote_copy(
            src_ref=src, dst_ref=dst, send_sem=send, recv_sem=recv, device_id=where, device_id_type=MESH
        )

    near_copies = [
        remote(pk_ref, near.at[n], near_send.at[n], near_recv.at[n], {"gz": to}) for n, to in enumerate((partner, other))
    ]

    def pair_z(slot, src):
        far_plane, far_side = odd * (nz - 1), 1 - odd
        near_plane, near_side = (1 - odd) * (nz - 1), odd
        return [
            remote(src.at[far_plane], halo_z.at[slot, far_side], hz_send.at[slot, 0], hz_recv.at[slot, 0], {"gz": other}),
            remote(
                src.at[near_plane], halo_z.at[slot, near_side], hz_send.at[slot, 1], hz_recv.at[slot, 1], {"gz": partner}
            ),
        ]

    def pair_y(slot, to_north, to_south, from_south, from_north):
        return (
            remote(to_north, from_south, hy_send.at[slot, 0], hy_recv.at[slot, 0], {"gy": north_gy}),
            remote(to_south, from_north, hy_send.at[slot, 1], hy_recv.at[slot, 1], {"gy": south_gy}),
        )

    def start_y(pair):
        north, south = pair

        @pl.when(has_n)
        def _():
            north.start()

        @pl.when(has_s)
        def _():
            south.start()

    def wait_y(pair):
        north, south = pair

        @pl.when(has_n)
        def _():
            north.wait_send()
            south.wait_recv()

        @pl.when(has_s)
        def _():
            south.wait_send()
            north.wait_recv()

    def start_z(pair):
        for c in pair:
            c.start()

    def wait_z(pair):
        for c in pair:
            c.wait()

    def tile_pair(slot, src):
        return pair_y(
            slot, src.at[:, pl.ds(ny - 8, 8), :], src.at[:, pl.ds(0, 8), :], halo_y.at[slot, 0], halo_y.at[slot, 1]
        )

    p_z, den_z, p_y, den_y = pair_z(0, p_ref), pair_z(1, den_ref), tile_pair(0, p_ref), tile_pair(1, den_ref)

    iota8 = lax.broadcasted_iota(jnp.int32, (8, LANES), 0).astype(F32)
    iota16 = lax.broadcasted_iota(jnp.int32, (16, LANES), 0).astype(F32)
    plane_id = (lax.broadcasted_iota(jnp.int32, (planes, LANES), 0) - HALO).astype(F32)
    south_end = jnp.where(has_s, 0, HALO).astype(F32)
    north_end = jnp.where(has_n, rows, rows - HALO).astype(F32)

    def masked(t, half):
        return jnp.where(jnp.abs(t) <= REACH, tap(t + half), 0.0)

    def split_blocks(home, size):
        block = jnp.floor(home * (1.0 / size))
        inner = home - block * size
        low = inner < size // 2
        return block, inner, jnp.where(low, block - 1.0, block + 1.0), jnp.where(low, -1.0 * size, 1.0 * size)

    def prepare(pk, brick, slot, at, width):
        for off in range(0, width, LANES):
            sl = pl.ds(pl.multiple_of(at + off, LANES), LANES)
            cz, cy, cx = [c.astype(F32) for c in split_cell(pk[4:5, sl].astype(jnp.int32), ny, nx)]
            hz, hy, hx = 0.5 - pk[5:6, sl], 0.5 - pk[6:7, sl], 0.5 - pk[7:8, sl]
            sum_z = jnp.sum(masked(iota8 - REACH, hz), axis=0, keepdims=True)
            wz_ref[slot, :, sl] = masked(plane_id - (cz + brick), hz) * (1.0 / sum_z)

            block, inner, beside, shift = split_blocks(cy + HALO, 8)
            t0 = iota8 - inner
            t1 = t0 + shift
            r0 = iota8 + block * 8
            r1 = iota8 + beside * 8
            v0 = jnp.where((r0 >= south_end) & (r0 < north_end), masked(t0, hy), 0.0)
            v1 = jnp.where((r1 >= south_end) & (r1 < north_end), masked(t1, hy), 0.0)
            scale = 1.0 / jnp.sum(v0 + v1, axis=0, keepdims=True)
            v0, v1 = v0 * scale, v1 * scale
            block, beside = jnp.broadcast_to(block, (8, LANES)), jnp.broadcast_to(beside, (8, LANES))
            for g in range(rows // 8):
                wy_ref[slot, 8 * g : 8 * g + 8, sl] = jnp.where(block == g, v0, jnp.where(beside == g, v1, 0.0))

            block, inner, beside, shift = split_blocks(cx, 16)
            t0 = iota16 - inner
            t1 = t0 + shift
            inside = (beside >= 0) & (beside < nx // 16)
            v0 = masked(t0, hx)
            v1 = jnp.where(inside, masked(t1, hx), 0.0)
            scale = 1.0 / jnp.sum(v0 + v1, axis=0, keepdims=True)
            v0, v1 = (v0 * scale).astype(jnp.bfloat16), (v1 * scale).astype(jnp.bfloat16)
            block = jnp.broadcast_to(block, (16, LANES)).astype(jnp.bfloat16)
            beside = jnp.broadcast_to(beside, (16, LANES)).astype(jnp.bfloat16)
            none = jnp.zeros((16, LANES), jnp.bfloat16)
            for g in range(nx // 16):
                wx_ref[slot, 16 * g : 16 * g + 16, sl] = jnp.where(block == g, v0, jnp.where(beside == g, v1, none))

    def deposit(pk, slot, lo, n, add, beside=None, after=None):
        def body(j, carry):
            i = lo + j
            acc = None
            for at in range(0, slots, CHUNK):
                sl = pl.ds(at, CHUNK)
                scaled = pk[0:4, sl] * wz_ref[slot, pl.ds(i, 1), sl]
                wy = wy_ref[slot, :, sl]
                lhs = jnp.concatenate([scaled[k : k + 1] * wy for k in range(4)], axis=0).astype(jnp.bfloat16)
                part = lax.dot_general(
                    lhs, wx_ref[slot, :, sl], (((1,), (1,)), ((), ())), preferred_element_type=F32
                )
                acc = part if acc is None else acc + part
                if beside is not None:
                    beside(j * (slots // CHUNK) + at // CHUNK)
            acc = acc.reshape(4, rows, nx)
            dep[i] = dep[i] + acc if add else acc
            if after is not None:
                after(i)
            return carry

        lax.fori_loop(0, n, body, 0)

    dep[0] = jnp.zeros((4, rows, nx), F32)
    dep[planes - 1] = jnp.zeros((4, rows, nx), F32)

    def prepare_all(pk, brick, slot):
        def body(i, carry):
            prepare(pk, brick, slot, i * 4 * LANES, 4 * LANES)
            return carry

        lax.fori_loop(0, slots // (4 * LANES), body, 0)

    prepare_all(pk_ref, 0.0, 0)
    reach = HALO + REACH
    side = (1 - 2 * odd).astype(F32) * nz
    lo_near, lo_far = (1 - odd) * (planes - reach), odd * (planes - reach)
    ahead = planes - 2 * (HALO - REACH) - nz
    deposit(pk_ref, 0, HALO - REACH, ahead, False)
    pl.semaphore_wait(barrier, count - 1)
    for c in near_copies:
        c.start()
    for c in loads[4:]:
        c.wait()
    start_y(den_y)
    start_y(p_y)
    deposit(pk_ref, 0, HALO - REACH + ahead, nz, False)

    def tile_pair_of(i):
        return (
            remote(
                dep.at[i, :, pl.ds(ny, EDGE), :], tile_in.at[0, i], tile_send.at[i, 0], tile_recv.at[i, 0],
                {"gy": north_gy},
            ),
            remote(
                dep.at[i, :, pl.ds(0, EDGE), :], tile_in.at[1, i], tile_send.at[i, 1], tile_recv.at[i, 1],
                {"gy": south_gy},
            ),
        )

    def send_tiles(i):
        start_y(tile_pair_of(i))

    near_copies[0].wait()
    prepare_all(near.at[0], side, 1)
    for i in range(reach, planes - reach):
        send_tiles(i)
    deposit(near.at[0], 1, lo_near, reach - 4, True, None, send_tiles)
    near_copies[1].wait()
    start_z(den_z)
    start_z(p_z)
    share = slots // (4 * (slots // CHUNK))

    def prepare_far(n):
        prepare(near.at[1], -side, 2, n * share, share)

    deposit(near.at[0], 1, lo_near + reach - 4, 4, True, prepare_far, send_tiles)
    deposit(near.at[1], 2, lo_far, reach, True, None, send_tiles)

    def add_tiles(lo, n):
        def body(j, carry):
            i = lo + j
            wait_y(tile_pair_of(i))

            @pl.when(has_s)
            def _():
                dep[i, :, 0:EDGE, :] = dep[i, :, 0:EDGE, :] + tile_in[0, i]

            @pl.when(has_n)
            def _():
                dep[i, :, ny : ny + EDGE, :] = dep[i, :, ny : ny + EDGE, :] + tile_in[1, i]

            return carry

        lax.fori_loop(0, n, body, 0)

    def shifts_x(v):
        lane = lax.broadcasted_iota(jnp.int32, (v.shape[0], LANES), 1)
        parts = [v[:, at : at + LANES] for at in range(0, nx, LANES)]
        ups = [pltpu.roll(part, 1, 1) for part in parts]
        downs = [pltpu.roll(part, LANES - 1, 1) for part in parts]
        west = [jnp.where(lane == 0, ups[n - 1] if n else 0.0, u) for n, u in enumerate(ups)]
        east = [
            jnp.where(lane == LANES - 1, downs[n + 1] if n + 1 < len(parts) else 0.0, u) for n, u in enumerate(downs)
        ]
        return jnp.concatenate(west, axis=1), jnp.concatenate(east, axis=1)

    def sweep(src, dst, lo, n):
        place = lax.broadcasted_iota(jnp.int32, (rows, nx), 0) - HALO + first
        lane = lax.broadcasted_iota(jnp.int32, (rows, nx), 1)
        count = (
            2.0
            + (place >= 1).astype(F32)
            + (place < total_y - 1).astype(F32)
            + (lane >= 1).astype(F32)
            + (lane < nx - 1).astype(F32)
        )
        inside = (place >= 0) & (place < total_y)
        scale_c = jnp.where(inside, 1.0 - smooth_rate * count, 0.0)
        scale_n = jnp.where(inside, smooth_rate, 0.0)

        def body(j, carry):
            i = lo + j
            for k in range(4):
                c = src[i, k]
                west, east = shifts_x(c)
                beside = (
                    src[i - 1, k] + src[i + 1, k] + pltpu.roll(c, 1, 0) + pltpu.roll(c, rows - 1, 0) + west + east
                )
                dst[i, k] = scale_c * c + scale_n * beside
            return carry

        lax.fori_loop(0, n, body, 0)

    half = planes // 2 - 1
    bufs = [dep, fld]
    add_tiles(lo_near + (odd - 1) * (planes - 2 * reach), planes - reach)
    sweep(dep, fld, 1 + (1 - odd) * half, half)
    add_tiles(lo_far, reach)
    sweep(dep, fld, 1 + odd * half, half)
    for s in range(1, SWEEPS):
        sweep(bufs[s % 2], bufs[(s + 1) % 2], s + 1, planes - 2 * s - 2)
    f = bufs[SWEEPS % 2]

    def own(v, shift=0):
        return pltpu.roll(v, rows - HALO - shift, 0)[0:ny]

    wait_y(den_y)
    wait_y(p_y)
    wait_z(den_z)
    wait_z(p_z)
    for z in range(-1, nz + 1):
        g = own(1.0 / (1.0 + f[z + HALO, 0]))
        if 0 <= z < nz:
            gf_ref[z] = g
            for k in range(3):
                mom_ref[z, k] = own(f[z + HALO, k + 1])
            den = den_ref[z]
        else:
            den = halo_z[1, 0 if z < 0 else 1]
        mob[z + 1] = g / den

    own_row = lax.broadcasted_iota(jnp.int32, (ny, nx), 0)

    def shifts_y(v, south_row, north_row):
        south = jnp.where(own_row == 0, south_row, pltpu.roll(v, 1, 0))
        north = jnp.where(own_row == ny - 1, north_row, pltpu.roll(v, ny - 1, 0))
        return south, north

    def halo_rows(slot, z):
        if slot < 2:
            south, north = halo_y[slot, 0, z, 7:8, :], halo_y[slot, 1, z, 0:1, :]
        else:
            south, north = edge_in[slot - 2, 0, z : z + 1, :], edge_in[slot - 2, 1, z : z + 1, :]
        return jnp.where(has_s, south, 0.0), jnp.where(has_n, north, 0.0)

    def apply(v, slot, z):
        c = v[z]
        below = v[z - 1] if z > 0 else halo_z[slot, 0]
        above = v[z + 1] if z < nz - 1 else halo_z[slot, 1]
        south, north = shifts_y(c, *halo_rows(slot, z))
        west, east = shifts_x(c)
        coupled = (
            face_z[z] * below + face_z[z + 1] * above + face_s[z] * south + face_n[z] * north
            + face_w[z] * west + face_e[z] * east
        )
        return diag[z] * c - coupled

    def keep_edge(slot, z, v):
        edge[slot, 0, z : z + 1, :] = v[ny - 1 : ny]
        edge[slot, 1, z : z + 1, :] = v[0:1]

    def edge_pair(slot):
        return pair_y(
            slot, edge.at[slot - 2, 0], edge.at[slot - 2, 1], edge_in.at[slot - 2, 0], edge_in.at[slot - 2, 1]
        )

    for z in range(nz + 1):
        face_z[z] = 0.5 * (mob[z] + mob[z + 1])
    order = [0, nz - 1] + list(range(1, nz - 1))
    inner_first = list(range(1, nz - 1)) + [0, nz - 1]
    z_z, w_z, z_y, w_y = pair_z(2, z_ref), pair_z(3, w_ref), edge_pair(2), edge_pair(3)
    for z in order:
        m = mob[z + 1]
        gs = f[z + HALO, 0, HALO - 1 : HALO, :]
        gn = f[z + HALO, 0, HALO + ny : HALO + ny + 1, :]
        ms = jnp.where(has_s, 1.0 / (1.0 + gs) / halo_y[1, 0, z, 7:8, :], 0.0)
        mn = jnp.where(has_n, 1.0 / (1.0 + gn) / halo_y[1, 1, z, 0:1, :], 0.0)
        south, north = shifts_y(m, ms, mn)
        west, east = shifts_x(m)
        fs, fn, fw, fe = 0.5 * (m + south), 0.5 * (m + north), 0.5 * (m + west), 0.5 * (m + east)
        face_s[z], face_n[z], face_w[z], face_e[z] = fs, fn, fw, fe
        dg = stiffness * m + face_z[z] + face_z[z + 1] + fs + fn + fw + fe
        diag[z] = dg
        mz_d, mz_u = own(f[z + HALO - 1, 1]), own(f[z + HALO + 1, 1])
        my = f[z + HALO, 2]
        xw, xe = shifts_x(own(f[z + HALO, 3]))
        spread = 0.5 * (mz_u - mz_d) + 0.5 * (own(my, 1) - own(my, -1)) + 0.5 * (xe - xw)
        r0 = div_ref[z] - spread - apply(p_ref, 0, z)
        r_ref[z] = r0
        z0 = r0 / dg
        z_ref[z] = z0
        keep_edge(0, z, z0)
        if z == nz - 1:
            start_z(z_z)
    start_y(z_y)

    def fold(v):
        part = jnp.sum(v, axis=0, keepdims=True)
        out = part[:, 0:LANES]
        for at in range(LANES, nx, LANES):
            out = out + part[:, at : at + LANES]
        for step in (64, 32):
            out = out + pltpu.roll(out, step, 1)
        return out

    sums = [jnp.zeros((ny, nx), F32)] * 4
    wait_y(z_y)
    for z in inner_first:
        if z == 0:
            wait_z(z_z)
        q = apply(z_ref, 2, z)
        w = q / diag[z]
        q_ref[z] = q
        w_ref[z] = w
        keep_edge(1, z, w)
    start_z(w_z)
    start_y(w_y)
    for z in range(nz):
        sums[0] = sums[0] + r_ref[z] * z_ref[z]
        sums[1] = sums[1] + z_ref[z] * q_ref[z]
        sums[2] = sums[2] + q_ref[z] * w_ref[z]
    wait_y(w_y)
    for z in inner_first:
        if z == 0:
            wait_z(w_z)
        aw = apply(w_ref, 3, z)
        aw_ref[z] = aw
        sums[3] = sums[3] + w_ref[z] * aw
    quarter = lax.broadcasted_iota(jnp.int32, (1, LANES), 1) // 32
    line = fold(sums[3])
    for n in range(3):
        line = jnp.where(quarter == n, fold(sums[n]), line)
    row_ref[0] = line

    def row_copy(d):
        return remote(row_ref.at[0], red.at[me], row_send.at[d - 1], row_recv.at[me], place_of(d))

    def row_from(d):
        whom = lax.rem(me + count - d, count)
        return remote(row_ref.at[0], red.at[whom], row_send.at[d - 1], row_recv.at[whom], place_of(d))

    each_other(lambda d: row_copy(d).start())
    red[me] = line
    each_other(lambda d: row_copy(d).wait_send())
    each_other(lambda d: row_from(d).wait_recv())
    total = jnp.sum(red[...], axis=0)
    norm0, curve0, mix, square = [
        jnp.sum(jnp.where(quarter == n, total, 0.0), axis=1, keepdims=True) for n in range(4)
    ]
    step0 = norm0 / curve0
    norm1 = norm0 - 2.0 * step0 * curve0 + step0 * step0 * mix
    curve1 = curve0 - 2.0 * step0 * mix + step0 * step0 * square
    beta = norm1 / norm0
    step1 = norm1 / (curve1 - beta * norm1 / step0)
    along, back = step0 + step1 * (1.0 + beta), step0 * step1
    for z in range(nz):
        out_ref[z] = p_ref[z] + along * z_ref[z] - back * w_ref[z]
        res_ref[z] = r_ref[z] - along * q_ref[z] + back * aw_ref[z]


def pass_kernel(*refs):
    ins, outs, put = refs[0:4], refs[4:8], refs[8]
    ways = [pltpu.make_async_copy(ins[n], outs[n], put.at[n]) for n in range(4)]
    for c in ways:
        c.start()
    for c in ways:
        c.wait()


def on_device(ngz, ngy, parcel_cell, parcel_offset, parcel_volume, parcel_force, brick_counts,
              divergence, pressure_prev, gas_density):
    nz, ny, nx = divergence.shape
    slots = parcel_cell.shape[0]
    planes, rows = nz + 2 * HALO, ny + EDGE
    field = jax.ShapeDtypeStruct((nz, ny, nx), F32)
    own = pltpu.VMEM((nz, ny, nx), F32)
    dma = pltpu.SemaphoreType.DMA
    vmem = pl.BlockSpec(memory_space=pltpu.VMEM)
    hbm = pl.BlockSpec(memory_space=pl.ANY)
    shapes = (field, jax.ShapeDtypeStruct((nz, 3, ny, nx), F32), field, field)
    count = ngz * ngy
    made = pl.pallas_call(
        functools.partial(step_kernel, ngz, ngy, nz, ny, nx, slots),
        out_shape=tuple(pltpu.VMEM(shape.shape, F32) for shape in shapes),
        in_specs=[pl.BlockSpec(memory_space=pltpu.SMEM)] + [hbm] * 7,
        out_specs=(vmem,) * 4,
        scratch_shapes=[
            pltpu.VMEM((1, slots), jnp.int32), pltpu.VMEM((3, slots), F32),
            pltpu.VMEM((1, slots), F32), pltpu.VMEM((3, slots), F32),
            own, own, own,
            pltpu.VMEM((8, slots), F32),
            pltpu.VMEM((2, 8, slots), F32),
            pltpu.VMEM((3, planes, slots), F32),
            pltpu.VMEM((3, rows, slots), F32),
            pltpu.VMEM((3, nx, slots), jnp.bfloat16),
            pltpu.VMEM((planes, 4, rows, nx), F32),
            pltpu.VMEM((planes, 4, rows, nx), F32),
            pltpu.VMEM((2, planes, 4, EDGE, nx), F32),
            pltpu.VMEM((4, 2, ny, nx), F32),
            pltpu.VMEM((2, 2, nz, 8, nx), F32),
            pltpu.VMEM((2, 2, nz, nx), F32),
            pltpu.VMEM((2, 2, nz, nx), F32),
            pltpu.VMEM((nz + 2, ny, nx), F32),
            pltpu.VMEM((nz + 1, ny, nx), F32),
            own, own, own, own, own,
            own, own, own, own, own,
            pltpu.VMEM((1, 1, 128), F32),
            pltpu.VMEM((count, 1, 128), F32),
            dma((7,)), dma((2,)), dma((2,)),
            dma((planes, 2)), dma((planes, 2)),
            dma((4, 2)), dma((4, 2)), dma((4, 2)), dma((4, 2)),
            dma((count,)), dma((count,)),
        ],
        compiler_params=pltpu.CompilerParams(
            collective_id=0, has_side_effects=True, vmem_limit_bytes=48 * 1024 * 1024
        ),
    )(brick_counts, *[
        pltpu.with_memory_space_constraint(array, pltpu.HBM)
        for array in (
            parcel_cell[None, :], parcel_offset, parcel_volume[None, :], parcel_force,
            divergence, pressure_prev, gas_density,
        )
    ])
    return pl.pallas_call(
        pass_kernel,
        out_shape=shapes,
        in_specs=[vmem] * 4,
        out_specs=(hbm,) * 4,
        scratch_shapes=[dma((4,))],
    )(*[pltpu.with_memory_space_constraint(array, pltpu.VMEM) for array in made])


def solution(mesh):
    ngz, ngy = mesh.shape["gz"], mesh.shape["gy"]
    return jax.shard_map(
        functools.partial(on_device, ngz, ngy),
        mesh=mesh,
        in_specs=(
            P(("gz", "gy")),
            P(None, ("gz", "gy")),
            P(("gz", "gy")),
            P(None, ("gz", "gy")),
            P("gz", "gy"),
            P("gz", "gy", None),
            P("gz", "gy", None),
            P("gz", "gy", None),
        ),
        out_specs=(
            P("gz", "gy", None),
            P("gz", None, "gy", None),
            P("gz", "gy", None),
            P("gz", "gy", None),
        ),
        check_vma=False,
    )
```

```python
import functools
import math

import jax
import jax.numpy as jnp
from jax import lax
from jax.experimental import pallas as pl
from jax.experimental.pallas import tpu as pltpu
from jax.sharding import PartitionSpec as P

SWEEPS = 3
REACH = 3
HALO = SWEEPS + 1
EDGE = 2 * HALO
CHUNK = 1024
LANES = 128
OWN_WIDE = 2
NEAR_WIDE = 2
BESIDE = 4
smooth_rate = 0.15
stiffness = 0.002
F32 = jnp.float32
MESH = pl.DeviceIdType.MESH


def tap(distance):
    return jnp.exp2((-0.5 * math.log2(math.e)) * (distance * distance))


def split_cell(cell, ny, nx):
    if ny & (ny - 1) == 0 and nx & (nx - 1) == 0:
        sx, sy = nx.bit_length() - 1, ny.bit_length() - 1
        return (
            lax.shift_right_logical(cell, sx + sy),
            lax.shift_right_logical(cell, sx) & (ny - 1),
            cell & (nx - 1),
        )
    row = lax.div(cell, nx)
    return lax.div(row, ny), lax.rem(row, ny), lax.rem(cell, nx)


def step_kernel(
    ngz, ngy, nz, ny, nx, slots,
    count_ref, cell_hbm, off_hbm, vol_hbm, force_hbm, div_hbm, p_hbm, den_hbm,
    gf_ref, mom_ref, out_ref, res_ref,
    cell_ref, off_ref, vol_ref, force_ref, div_ref, p_ref, den_ref, pk_ref, near, wz_ref, wy_ref, wx_ref, dep, fld, tile_in,
    halo_z, halo_y, edge, edge_in, mob, face_z, face_s, face_n, face_w, face_e, diag,
    r_ref, z_ref, q_ref, w_ref, aw_ref, row_ref, red,
    load_sem, near_send, near_recv, tile_send, tile_recv, hz_send, hz_recv, hy_send, hy_recv,
    row_send, row_recv,
):
    gz, gy = lax.axis_index("gz"), lax.axis_index("gy")
    planes, rows = nz + 2 * HALO, ny + EDGE
    total_y = ngy * ny
    first = gy * ny
    count = ngz * ngy
    me = gz * ngy + gy
    odd = lax.rem(gz, 2)
    up, down = lax.rem(gz + 1, ngz), lax.rem(gz + ngz - 1, ngz)
    partner, other = jnp.where(odd == 1, down, up), jnp.where(odd == 1, up, down)
    north_gy, south_gy = lax.rem(gy + 1, ngy), lax.rem(gy + ngy - 1, ngy)
    has_s, has_n = gy > 0, gy < ngy - 1

    loads = [
        pltpu.make_async_copy(src, dst, load_sem.at[n])
        for n, (src, dst) in enumerate((
            (cell_hbm, cell_ref), (off_hbm, off_ref), (vol_hbm, vol_ref), (force_hbm, force_ref),
            (den_hbm, den_ref), (p_hbm, p_ref), (div_hbm, div_ref),
        ))
    ]
    for c in loads:
        c.start()

    def place_of(d):
        to = lax.rem(me + d, count)
        to_z = lax.div(to, ngy)
        return {"gz": to_z, "gy": to - to_z * ngy}

    def each_other(body):
        if count <= 64:
            for d in range(1, count):
                body(d)
        else:
            lax.fori_loop(1, count, lambda d, carry: (body(d), carry)[1], 0)

    barrier = pltpu.get_barrier_semaphore()
    each_other(lambda d: pl.semaphore_signal(barrier, inc=1, device_id=place_of(d), device_id_type=MESH))

    for c in loads[:4]:
        c.wait()
    live = lax.broadcasted_iota(jnp.int32, (1, slots), 1) < count_ref[0, 0]
    volume = jnp.where(live, vol_ref[...], 0.0)
    pk_ref[0:1] = volume
    pk_ref[1:4] = volume * force_ref[...]
    pk_ref[4:5] = cell_ref[...].astype(F32)
    pk_ref[5:8] = off_ref[...]

    def remote(src, dst, send, recv, where):
        return pltpu.make_async_remote_copy(
            src_ref=src, dst_ref=dst, send_sem=send, recv_sem=recv, device_id=where, device_id_type=MESH
        )

    near_copies = [
        remote(pk_ref, near.at[n], near_send.at[n], near_recv.at[n], {"gz": to}) for n, to in enumerate((partner, other))
    ]

    def pair_z(slot, src):
        far_plane, far_side = odd * (nz - 1), 1 - odd
        near_plane, near_side = (1 - odd) * (nz - 1), odd
        return [
            remote(src.at[far_plane], halo_z.at[slot, far_side], hz_send.at[slot, 0], hz_recv.at[slot, 0], {"gz": other}),
            remote(
                src.at[near_plane], halo_z.at[slot, near_side], hz_send.at[slot, 1], hz_recv.at[slot, 1], {"gz": partner}
            ),
        ]

    def pair_y(slot, to_north, to_south, from_south, from_north):
        return (
            remote(to_north, from_south, hy_send.at[slot, 0], hy_recv.at[slot, 0], {"gy": north_gy}),
            remote(to_south, from_north, hy_send.at[slot, 1], hy_recv.at[slot, 1], {"gy": south_gy}),
        )

    def start_y(pair):
        north, south = pair

        @pl.when(has_n)
        def _():
            north.start()

        @pl.when(has_s)
        def _():
            south.start()

    def wait_y(pair):
        north, south = pair

        @pl.when(has_n)
        def _():
            north.wait_send()
            south.wait_recv()

        @pl.when(has_s)
        def _():
            south.wait_send()
            north.wait_recv()

    def start_z(pair):
        for c in pair:
            c.start()

    def wait_z(pair):
        for c in pair:
            c.wait()

    def tile_pair(slot, src):
        return pair_y(
            slot, src.at[:, pl.ds(ny - 8, 8), :], src.at[:, pl.ds(0, 8), :], halo_y.at[slot, 0], halo_y.at[slot, 1]
        )

    p_z, den_z, p_y, den_y = pair_z(0, p_ref), pair_z(1, den_ref), tile_pair(0, p_ref), tile_pair(1, den_ref)

    iota8 = lax.broadcasted_iota(jnp.int32, (8, LANES), 0).astype(F32)
    iota16 = lax.broadcasted_iota(jnp.int32, (16, LANES), 0).astype(F32)
    plane_id = (lax.broadcasted_iota(jnp.int32, (planes, LANES), 0) - HALO).astype(F32)
    south_end = jnp.where(has_s, 0, HALO).astype(F32)
    north_end = jnp.where(has_n, rows, rows - HALO).astype(F32)

    def masked(t, half):
        return jnp.where(jnp.abs(t) <= REACH, tap(t + half), 0.0)

    def split_blocks(home, size):
        block = jnp.floor(home * (1.0 / size))
        inner = home - block * size
        low = inner < size // 2
        return block, inner, jnp.where(low, block - 1.0, block + 1.0), jnp.where(low, -1.0 * size, 1.0 * size)

    def prepare(pk, brick, slot, at, width):
        for off in range(0, width, LANES):
            sl = pl.ds(pl.multiple_of(at + off, LANES), LANES)
            cz, cy, cx = [c.astype(F32) for c in split_cell(pk[4:5, sl].astype(jnp.int32), ny, nx)]
            hz, hy, hx = 0.5 - pk[5:6, sl], 0.5 - pk[6:7, sl], 0.5 - pk[7:8, sl]
            sum_z = jnp.sum(masked(iota8 - REACH, hz), axis=0, keepdims=True)
            wz_ref[slot, :, sl] = masked(plane_id - (cz + brick), hz) * (1.0 / sum_z)

            block, inner, beside, shift = split_blocks(cy + HALO, 8)
            t0 = iota8 - inner
            t1 = t0 + shift
            r0 = iota8 + block * 8
            r1 = iota8 + beside * 8
            v0 = jnp.where((r0 >= south_end) & (r0 < north_end), masked(t0, hy), 0.0)
            v1 = jnp.where((r1 >= south_end) & (r1 < north_end), masked(t1, hy), 0.0)
            scale = 1.0 / jnp.sum(v0 + v1, axis=0, keepdims=True)
            v0, v1 = v0 * scale, v1 * scale
            block, beside = jnp.broadcast_to(block, (8, LANES)), jnp.broadcast_to(beside, (8, LANES))
            for g in range(rows // 8):
                wy_ref[slot, 8 * g : 8 * g + 8, sl] = jnp.where(block == g, v0, jnp.where(beside == g, v1, 0.0))

            block, inner, beside, shift = split_blocks(cx, 16)
            t0 = iota16 - inner
            t1 = t0 + shift
            inside = (beside >= 0) & (beside < nx // 16)
            v0 = masked(t0, hx)
            v1 = jnp.where(inside, masked(t1, hx), 0.0)
            scale = 1.0 / jnp.sum(v0 + v1, axis=0, keepdims=True)
            v0, v1 = (v0 * scale).astype(jnp.bfloat16), (v1 * scale).astype(jnp.bfloat16)
            block = jnp.broadcast_to(block, (16, LANES)).astype(jnp.bfloat16)
            beside = jnp.broadcast_to(beside, (16, LANES)).astype(jnp.bfloat16)
            none = jnp.zeros((16, LANES), jnp.bfloat16)
            for g in range(nx // 16):
                wx_ref[slot, 16 * g : 16 * g + 16, sl] = jnp.where(block == g, v0, jnp.where(beside == g, v1, none))

    def deposit(pk, slot, lo, n, add, wide=1, beside=None, after=None, parts=4):
        assert n % wide == 0

        def body(j, carry):
            i = lo + j * wide
            acc = None
            for at in range(0, slots, CHUNK):
                sl = pl.ds(at, CHUNK)
                wy = wy_ref[slot, :, sl]
                stack = []
                for h in range(wide):
                    scaled = pk[0:parts, sl] * wz_ref[slot, pl.ds(i + h, 1), sl]
                    stack += [scaled[k : k + 1] * wy for k in range(parts)]
                lhs = jnp.concatenate(stack, axis=0).astype(jnp.bfloat16)
                part = lax.dot_general(
                    lhs, wx_ref[slot, :, sl], (((1,), (1,)), ((), ())), preferred_element_type=F32
                )
                acc = part if acc is None else acc + part
                if beside is not None:
                    beside(j * (slots // CHUNK) + at // CHUNK)
            acc = acc.reshape(wide, parts, rows, nx)
            for h in range(wide):
                dep[i + h, 0:parts] = dep[i + h, 0:parts] + acc[h] if add else acc[h]
                if after is not None:
                    after(i + h)
            return carry

        lax.fori_loop(0, n // wide, body, 0)

    dep[0] = jnp.zeros((4, rows, nx), F32)
    dep[planes - 1] = jnp.zeros((4, rows, nx), F32)

    def prepare_all(pk, brick, slot):
        def body(i, carry):
            prepare(pk, brick, slot, i * 4 * LANES, 4 * LANES)
            return carry

        lax.fori_loop(0, slots // (4 * LANES), body, 0)

    prepare_all(pk_ref, 0.0, 0)
    reach = HALO + REACH
    side = (1 - 2 * odd).astype(F32) * nz
    lo_near, lo_far = (1 - odd) * (planes - reach), odd * (planes - reach)
    out_near, out_far = (1 - odd) * (planes - 1), odd * (planes - 1)
    reached = nz + 2 * REACH
    ahead = 4
    deposit(pk_ref, 0, HALO - REACH, ahead, False, OWN_WIDE)
    pl.semaphore_wait(barrier, count - 1)
    for c in near_copies:
        c.start()
    for c in loads[4:]:
        c.wait()
    start_y(den_y)
    start_y(p_y)
    deposit(pk_ref, 0, HALO - REACH + ahead, reached - ahead, False, OWN_WIDE)

    def tile_pair_of(i):
        return (
            remote(
                dep.at[i, :, pl.ds(ny, EDGE), :], tile_in.at[0, i], tile_send.at[i, 0], tile_recv.at[i, 0],
                {"gy": north_gy},
            ),
            remote(
                dep.at[i, :, pl.ds(0, EDGE), :], tile_in.at[1, i], tile_send.at[i, 1], tile_recv.at[i, 1],
                {"gy": south_gy},
            ),
        )

    def send_tiles(i):
        start_y(tile_pair_of(i))

    near_copies[0].wait()
    prepare_all(near.at[0], side, 1)
    for i in range(reach, planes - reach):
        send_tiles(i)
    deposit(near.at[0], 1, out_near, 1, True, 1, None, send_tiles, 2)
    early = reach - 1 - BESIDE
    deposit(near.at[0], 1, lo_near + odd, early, True, NEAR_WIDE, None, send_tiles)
    near_copies[1].wait()
    start_z(den_z)
    start_z(p_z)
    share = slots // (BESIDE // NEAR_WIDE * (slots // CHUNK))

    def prepare_far(n):
        prepare(near.at[1], -side, 2, n * share, share)

    deposit(near.at[0], 1, lo_near + odd + early, BESIDE, True, NEAR_WIDE, prepare_far, send_tiles)
    deposit(near.at[1], 2, out_far, 1, True, 1, None, send_tiles, 2)
    deposit(near.at[1], 2, lo_far + 1 - odd, reach - 1, True, NEAR_WIDE, None, send_tiles)

    def add_tiles(lo, n):
        def body(j, carry):
            i = lo + j
            wait_y(tile_pair_of(i))

            @pl.when(has_s)
            def _():
                dep[i, :, 0:EDGE, :] = dep[i, :, 0:EDGE, :] + tile_in[0, i]

            @pl.when(has_n)
            def _():
                dep[i, :, ny : ny + EDGE, :] = dep[i, :, ny : ny + EDGE, :] + tile_in[1, i]

            @pl.when(jnp.logical_not(has_s))
            def _():
                dep[i, :, HALO - 1 : HALO, :] = dep[i, :, HALO : HALO + 1, :]

            @pl.when(jnp.logical_not(has_n))
            def _():
                dep[i, :, HALO + ny : HALO + ny + 1, :] = dep[i, :, HALO + ny - 1 : HALO + ny, :]

            return carry

        lax.fori_loop(0, n, body, 0)

    def shifts_x(v, mirror=False):
        lane = lax.broadcasted_iota(jnp.int32, (v.shape[0], LANES), 1)
        parts = [v[:, at : at + LANES] for at in range(0, nx, LANES)]
        ups = [pltpu.roll(part, 1, 1) for part in parts]
        downs = [pltpu.roll(part, LANES - 1, 1) for part in parts]
        first_wall, last_wall = (parts[0], parts[-1]) if mirror else (0.0, 0.0)
        west = [jnp.where(lane == 0, ups[n - 1] if n else first_wall, u) for n, u in enumerate(ups)]
        east = [
            jnp.where(lane == LANES - 1, downs[n + 1] if n + 1 < len(parts) else last_wall, u)
            for n, u in enumerate(downs)
        ]
        return jnp.concatenate(west, axis=1), jnp.concatenate(east, axis=1)

    def sweep(src, dst, lo, n, last=False, ks=(0, 1, 2, 3)):
        sub = lax.broadcasted_iota(jnp.int32, (8, nx), 0)
        south_ghost = (sub == HALO - 1) & jnp.logical_not(has_s)
        north_ghost = (sub == (HALO + ny) % 8) & jnp.logical_not(has_n)

        def body(j, carry):
            i = lo + j
            for k in ks:

                def turned(t):
                    c = src[i, k, 8 * t : 8 * t + 8, :]
                    return c, pltpu.roll(c, 1, 0), pltpu.roll(c, 7, 0)

                lower, here = None, turned(0)
                for t in range(rows // 8):
                    upper = turned(t + 1) if t + 1 < rows // 8 else None
                    c, south, north = here
                    south = south if lower is None else jnp.where(sub == 0, lower[1], south)
                    north = north if upper is None else jnp.where(sub == 7, upper[2], north)
                    west, east = shifts_x(c, True)
                    at = slice(8 * t, 8 * t + 8)
                    beside = (src[i - 1, k, at, :] + src[i + 1, k, at, :]) + (south + north) + (west + east)
                    out = (1.0 - 6.0 * smooth_rate) * c + smooth_rate * beside
                    if t == 0:
                        out = jnp.where(south_ghost, 0.0 if last else pltpu.roll(out, 7, 0), out)
                    if upper is None:
                        out = jnp.where(north_ghost, 0.0 if last else pltpu.roll(out, 1, 0), out)
                    dst[i, k, at, :] = out
                    lower, here = here, upper
            return carry

        lax.fori_loop(0, n, body, 0)

    outer = (0, 1)
    half = planes // 2 - 2
    bufs = [dep, fld]
    add_tiles(lo_near + (odd - 1) * (planes - 2 * reach), planes - reach)
    sweep(dep, fld, odd + (1 - odd) * (planes - 2), 1, False, outer)
    sweep(dep, fld, 2 + (1 - odd) * half, half)
    add_tiles(lo_far, reach)
    sweep(dep, fld, 2 + odd * half, half)
    sweep(dep, fld, (1 - odd) + odd * (planes - 2), 1, False, outer)
    for s in range(1, SWEEPS - 1):
        for edge_plane in (s + 1, planes - s - 2):
            sweep(bufs[s % 2], bufs[(s + 1) % 2], edge_plane, 1, False, outer)
        sweep(bufs[s % 2], bufs[(s + 1) % 2], s + 2, planes - 2 * s - 4)
    before, f = bufs[(SWEEPS - 1) % 2], bufs[SWEEPS % 2]
    for edge_plane, inner_plane in ((HALO - 1, HALO), (HALO + nz, HALO + nz - 2)):
        sweep(before, f, edge_plane, 1, True, outer)
        sweep(before, f, inner_plane, 2, True)

    def own(v, shift=0):
        return pltpu.roll(v, rows - HALO - shift, 0)[0:ny]

    wait_y(den_y)
    wait_y(p_y)
    wait_z(den_z)
    wait_z(p_z)
    def mobility(z):
        g = own(1.0 / (1.0 + f[z + HALO, 0]))
        if 0 <= z < nz:
            gf_ref[z] = g
            for k in range(3):
                mom_ref[z, k] = own(f[z + HALO, k + 1])
            den = den_ref[z]
        else:
            den = halo_z[1, 0 if z < 0 else 1]
        mob[z + 1] = g / den

    own_row = lax.broadcasted_iota(jnp.int32, (ny, nx), 0)

    def shifts_y(v, south_row, north_row):
        south = jnp.where(own_row == 0, south_row, pltpu.roll(v, 1, 0))
        north = jnp.where(own_row == ny - 1, north_row, pltpu.roll(v, ny - 1, 0))
        return south, north

    def halo_rows(slot, z):
        if slot < 2:
            south, north = halo_y[slot, 0, z, 7:8, :], halo_y[slot, 1, z, 0:1, :]
        else:
            south, north = edge_in[slot - 2, 0, z : z + 1, :], edge_in[slot - 2, 1, z : z + 1, :]
        return jnp.where(has_s, south, 0.0), jnp.where(has_n, north, 0.0)

    def apply(v, slot, z):
        c = v[z]
        below = v[z - 1] if z > 0 else halo_z[slot, 0]
        above = v[z + 1] if z < nz - 1 else halo_z[slot, 1]
        south, north = shifts_y(c, *halo_rows(slot, z))
        west, east = shifts_x(c)
        coupled = (
            face_z[z] * below + face_z[z + 1] * above + face_s[z] * south + face_n[z] * north
            + face_w[z] * west + face_e[z] * east
        )
        return diag[z] * c - coupled

    def keep_edge(slot, z, v):
        edge[slot, 0, z : z + 1, :] = v[ny - 1 : ny]
        edge[slot, 1, z : z + 1, :] = v[0:1]

    def edge_pair(slot):
        return pair_y(
            slot, edge.at[slot - 2, 0], edge.at[slot - 2, 1], edge_in.at[slot - 2, 0], edge_in.at[slot - 2, 1]
        )

    inner_first = list(range(1, nz - 1)) + [0, nz - 1]
    z_z, w_z, z_y, w_y = pair_z(2, z_ref), pair_z(3, w_ref), edge_pair(2), edge_pair(3)
    def source(z):
        for side_z in (z, z + 1):
            face_z[side_z] = 0.5 * (mob[side_z] + mob[side_z + 1])
        m = mob[z + 1]
        gs = f[z + HALO, 0, HALO - 1 : HALO, :]
        gn = f[z + HALO, 0, HALO + ny : HALO + ny + 1, :]
        ms = jnp.where(has_s, 1.0 / (1.0 + gs) / halo_y[1, 0, z, 7:8, :], 0.0)
        mn = jnp.where(has_n, 1.0 / (1.0 + gn) / halo_y[1, 1, z, 0:1, :], 0.0)
        south, north = shifts_y(m, ms, mn)
        west, east = shifts_x(m)
        fs, fn, fw, fe = 0.5 * (m + south), 0.5 * (m + north), 0.5 * (m + west), 0.5 * (m + east)
        face_s[z], face_n[z], face_w[z], face_e[z] = fs, fn, fw, fe
        dg = stiffness * m + face_z[z] + face_z[z + 1] + fs + fn + fw + fe
        diag[z] = dg
        mz_d, mz_u = own(f[z + HALO - 1, 1]), own(f[z + HALO + 1, 1])
        my = f[z + HALO, 2]
        xw, xe = shifts_x(own(f[z + HALO, 3]))
        spread = 0.5 * (mz_u - mz_d) + 0.5 * (own(my, 1) - own(my, -1)) + 0.5 * (xe - xw)
        r0 = div_ref[z] - spread - apply(p_ref, 0, z)
        r_ref[z] = r0
        z0 = r0 / dg
        z_ref[z] = z0
        keep_edge(0, z, z0)

    for z in (-1, 0, 1, nz - 2, nz - 1, nz):
        mobility(z)
    for z in (0, nz - 1):
        source(z)
    start_z(z_z)
    sweep(before, f, HALO + 2, nz - 4, True)
    for z in range(2, nz - 2):
        mobility(z)
    for z in range(1, nz - 1):
        source(z)
    start_y(z_y)

    def fold(v):
        part = jnp.sum(v, axis=0, keepdims=True)
        out = part[:, 0:LANES]
        for at in range(LANES, nx, LANES):
            out = out + part[:, at : at + LANES]
        for step in (64, 32):
            out = out + pltpu.roll(out, step, 1)
        return out

    sums = [jnp.zeros((ny, nx), F32)] * 4
    wait_y(z_y)
    for z in inner_first:
        if z == 0:
            wait_z(z_z)
        q = apply(z_ref, 2, z)
        w = q / diag[z]
        q_ref[z] = q
        w_ref[z] = w
        keep_edge(1, z, w)
    start_z(w_z)
    start_y(w_y)
    for z in range(nz):
        sums[0] = sums[0] + r_ref[z] * z_ref[z]
        sums[1] = sums[1] + z_ref[z] * q_ref[z]
        sums[2] = sums[2] + q_ref[z] * w_ref[z]
    wait_y(w_y)
    for z in inner_first:
        if z == 0:
            wait_z(w_z)
        aw = apply(w_ref, 3, z)
        aw_ref[z] = aw
        sums[3] = sums[3] + w_ref[z] * aw
    quarter = lax.broadcasted_iota(jnp.int32, (1, LANES), 1) // 32
    line = fold(sums[3])
    for n in range(3):
        line = jnp.where(quarter == n, fold(sums[n]), line)
    row_ref[0] = line

    def row_copy(d):
        return remote(row_ref.at[0], red.at[me], row_send.at[d - 1], row_recv.at[me], place_of(d))

    def row_from(d):
        whom = lax.rem(me + count - d, count)
        return remote(row_ref.at[0], red.at[whom], row_send.at[d - 1], row_recv.at[whom], place_of(d))

    each_other(lambda d: row_copy(d).start())
    red[me] = line
    each_other(lambda d: row_copy(d).wait_send())
    each_other(lambda d: row_from(d).wait_recv())
    total = jnp.sum(red[...], axis=0)
    norm0, curve0, mix, square = [
        jnp.sum(jnp.where(quarter == n, total, 0.0), axis=1, keepdims=True) for n in range(4)
    ]
    step0 = norm0 / curve0
    norm1 = norm0 - 2.0 * step0 * curve0 + step0 * step0 * mix
    curve1 = curve0 - 2.0 * step0 * mix + step0 * step0 * square
    beta = norm1 / norm0
    step1 = norm1 / (curve1 - beta * norm1 / step0)
    along, back = step0 + step1 * (1.0 + beta), step0 * step1
    for z in range(nz):
        out_ref[z] = p_ref[z] + along * z_ref[z] - back * w_ref[z]
        res_ref[z] = r_ref[z] - along * q_ref[z] + back * aw_ref[z]


def pass_kernel(*refs):
    ins, outs, put = refs[0:4], refs[4:8], refs[8]
    ways = [pltpu.make_async_copy(ins[n], outs[n], put.at[n]) for n in range(4)]
    for c in ways:
        c.start()
    for c in ways:
        c.wait()


def on_device(ngz, ngy, parcel_cell, parcel_offset, parcel_volume, parcel_force, brick_counts,
              divergence, pressure_prev, gas_density):
    nz, ny, nx = divergence.shape
    slots = parcel_cell.shape[0]
    planes, rows = nz + 2 * HALO, ny + EDGE
    field = jax.ShapeDtypeStruct((nz, ny, nx), F32)
    own = pltpu.VMEM((nz, ny, nx), F32)
    dma = pltpu.SemaphoreType.DMA
    vmem = pl.BlockSpec(memory_space=pltpu.VMEM)
    hbm = pl.BlockSpec(memory_space=pl.ANY)
    shapes = (field, jax.ShapeDtypeStruct((nz, 3, ny, nx), F32), field, field)
    count = ngz * ngy
    made = pl.pallas_call(
        functools.partial(step_kernel, ngz, ngy, nz, ny, nx, slots),
        out_shape=tuple(pltpu.VMEM(shape.shape, F32) for shape in shapes),
        in_specs=[pl.BlockSpec(memory_space=pltpu.SMEM)] + [hbm] * 7,
        out_specs=(vmem,) * 4,
        scratch_shapes=[
            pltpu.VMEM((1, slots), jnp.int32), pltpu.VMEM((3, slots), F32),
            pltpu.VMEM((1, slots), F32), pltpu.VMEM((3, slots), F32),
            own, own, own,
            pltpu.VMEM((8, slots), F32),
            pltpu.VMEM((2, 8, slots), F32),
            pltpu.VMEM((3, planes, slots), F32),
            pltpu.VMEM((3, rows, slots), F32),
            pltpu.VMEM((3, nx, slots), jnp.bfloat16),
            pltpu.VMEM((planes, 4, rows, nx), F32),
            pltpu.VMEM((planes, 4, rows, nx), F32),
            pltpu.VMEM((2, planes, 4, EDGE, nx), F32),
            pltpu.VMEM((4, 2, ny, nx), F32),
            pltpu.VMEM((2, 2, nz, 8, nx), F32),
            pltpu.VMEM((2, 2, nz, nx), F32),
            pltpu.VMEM((2, 2, nz, nx), F32),
            pltpu.VMEM((nz + 2, ny, nx), F32),
            pltpu.VMEM((nz + 1, ny, nx), F32),
            own, own, own, own, own,
            own, own, own, own, own,
            pltpu.VMEM((1, 1, 128), F32),
            pltpu.VMEM((count, 1, 128), F32),
            dma((7,)), dma((2,)), dma((2,)),
            dma((planes, 2)), dma((planes, 2)),
            dma((4, 2)), dma((4, 2)), dma((4, 2)), dma((4, 2)),
            dma((count,)), dma((count,)),
        ],
        compiler_params=pltpu.CompilerParams(
            collective_id=0, has_side_effects=True, vmem_limit_bytes=48 * 1024 * 1024
        ),
    )(brick_counts, *[
        pltpu.with_memory_space_constraint(array, pltpu.HBM)
        for array in (
            parcel_cell[None, :], parcel_offset, parcel_volume[None, :], parcel_force,
            divergence, pressure_prev, gas_density,
        )
    ])
    return pl.pallas_call(
        pass_kernel,
        out_shape=shapes,
        in_specs=[vmem] * 4,
        out_specs=(hbm,) * 4,
        scratch_shapes=[dma((4,))],
    )(*[pltpu.with_memory_space_constraint(array, pltpu.VMEM) for array in made])


def solution(mesh):
    ngz, ngy = mesh.shape["gz"], mesh.shape["gy"]
    return jax.shard_map(
        functools.partial(on_device, ngz, ngy),
        mesh=mesh,
        in_specs=(
            P(("gz", "gy")),
            P(None, ("gz", "gy")),
            P(("gz", "gy")),
            P(None, ("gz", "gy")),
            P("gz", "gy"),
            P("gz", "gy", None),
            P("gz", "gy", None),
            P("gz", "gy", None),
        ),
        out_specs=(
            P("gz", "gy", None),
            P("gz", None, "gy", None),
            P("gz", "gy", None),
            P("gz", "gy", None),
        ),
        check_vma=False,
    )
```

```python
import functools
import math

import jax
import jax.numpy as jnp
from jax import lax
from jax.experimental import pallas as pl
from jax.experimental.pallas import tpu as pltpu
from jax.sharding import PartitionSpec as P

SWEEPS = 3
REACH = 3
HALO = SWEEPS + 1
EDGE = 2 * HALO
CHUNK = 1024
LANES = 128
OWN_WIDE = 2
NEAR_WIDE = 2
smooth_rate = 0.15
stiffness = 0.002
F32 = jnp.float32
MESH = pl.DeviceIdType.MESH


def tap(distance):
    return jnp.exp2((-0.5 * math.log2(math.e)) * (distance * distance))


def split_cell(cell, ny, nx):
    if ny & (ny - 1) == 0 and nx & (nx - 1) == 0:
        sx, sy = nx.bit_length() - 1, ny.bit_length() - 1
        return (
            lax.shift_right_logical(cell, sx + sy),
            lax.shift_right_logical(cell, sx) & (ny - 1),
            cell & (nx - 1),
        )
    row = lax.div(cell, nx)
    return lax.div(row, ny), lax.rem(row, ny), lax.rem(cell, nx)


def step_kernel(
    ngz, ngy, nz, ny, nx, slots,
    count_ref, cell_hbm, off_hbm, vol_hbm, force_hbm, div_hbm, p_hbm, den_hbm,
    gf_ref, mom_ref, out_ref, res_ref,
    cell_ref, off_ref, vol_ref, force_ref, div_ref, p_ref, den_ref, pk_ref, near, wz_ref, wy_ref, wx_ref, dep, fld, tile_in,
    halo_z, halo_y, edge, edge_in, mob, face_z, face_s, face_n, face_w, face_e, diag,
    r_ref, z_ref, q_ref, w_ref, aw_ref, row_ref, red,
    load_sem, near_send, near_recv, tile_send, tile_recv, hz_send, hz_recv, hy_send, hy_recv,
    row_send, row_recv,
):
    gz, gy = lax.axis_index("gz"), lax.axis_index("gy")
    planes, rows = nz + 2 * HALO, ny + EDGE
    total_y = ngy * ny
    first = gy * ny
    count = ngz * ngy
    me = gz * ngy + gy
    odd = lax.rem(gz, 2)
    up, down = lax.rem(gz + 1, ngz), lax.rem(gz + ngz - 1, ngz)
    partner, other = jnp.where(odd == 1, down, up), jnp.where(odd == 1, up, down)
    north_gy, south_gy = lax.rem(gy + 1, ngy), lax.rem(gy + ngy - 1, ngy)
    has_s, has_n = gy > 0, gy < ngy - 1

    loads = [
        pltpu.make_async_copy(src, dst, load_sem.at[n])
        for n, (src, dst) in enumerate((
            (cell_hbm, cell_ref), (off_hbm, off_ref), (vol_hbm, vol_ref), (force_hbm, force_ref),
            (den_hbm, den_ref), (p_hbm, p_ref), (div_hbm, div_ref),
        ))
    ]
    for c in loads:
        c.start()

    def place_of(d):
        to = lax.rem(me + d, count)
        to_z = lax.div(to, ngy)
        return {"gz": to_z, "gy": to - to_z * ngy}

    def each_other(body):
        if count <= 64:
            for d in range(1, count):
                body(d)
        else:
            lax.fori_loop(1, count, lambda d, carry: (body(d), carry)[1], 0)

    barrier = pltpu.get_barrier_semaphore()
    each_other(lambda d: pl.semaphore_signal(barrier, inc=1, device_id=place_of(d), device_id_type=MESH))

    for c in loads[:4]:
        c.wait()
    live = lax.broadcasted_iota(jnp.int32, (1, slots), 1) < count_ref[0, 0]
    volume = jnp.where(live, vol_ref[...], 0.0)
    pk_ref[0:1] = volume
    pk_ref[1:4] = volume * force_ref[...]
    pk_ref[4:5] = cell_ref[...].astype(F32)
    pk_ref[5:8] = off_ref[...]

    def remote(src, dst, send, recv, where):
        return pltpu.make_async_remote_copy(
            src_ref=src, dst_ref=dst, send_sem=send, recv_sem=recv, device_id=where, device_id_type=MESH
        )

    near_copies = [
        remote(pk_ref, near.at[n], near_send.at[n], near_recv.at[n], {"gz": to}) for n, to in enumerate((partner, other))
    ]

    def pair_z(slot, src):
        far_plane, far_side = odd * (nz - 1), 1 - odd
        near_plane, near_side = (1 - odd) * (nz - 1), odd
        return [
            remote(src.at[far_plane], halo_z.at[slot, far_side], hz_send.at[slot, 0], hz_recv.at[slot, 0], {"gz": other}),
            remote(
                src.at[near_plane], halo_z.at[slot, near_side], hz_send.at[slot, 1], hz_recv.at[slot, 1], {"gz": partner}
            ),
        ]

    def pair_y(slot, to_north, to_south, from_south, from_north):
        return (
            remote(to_north, from_south, hy_send.at[slot, 0], hy_recv.at[slot, 0], {"gy": north_gy}),
            remote(to_south, from_north, hy_send.at[slot, 1], hy_recv.at[slot, 1], {"gy": south_gy}),
        )

    def start_y(pair):
        north, south = pair

        @pl.when(has_n)
        def _():
            north.start()

        @pl.when(has_s)
        def _():
            south.start()

    def wait_y(pair):
        north, south = pair

        @pl.when(has_n)
        def _():
            north.wait_send()
            south.wait_recv()

        @pl.when(has_s)
        def _():
            south.wait_send()
            north.wait_recv()

    def start_z(pair):
        for c in pair:
            c.start()

    def wait_z(pair):
        for c in pair:
            c.wait()

    def tile_pair(slot, src):
        return pair_y(
            slot, src.at[:, pl.ds(ny - 8, 8), :], src.at[:, pl.ds(0, 8), :], halo_y.at[slot, 0], halo_y.at[slot, 1]
        )

    p_z, den_z, p_y, den_y = pair_z(0, p_ref), pair_z(1, den_ref), tile_pair(0, p_ref), tile_pair(1, den_ref)

    iota8 = lax.broadcasted_iota(jnp.int32, (8, LANES), 0).astype(F32)
    iota16 = lax.broadcasted_iota(jnp.int32, (16, LANES), 0).astype(F32)
    plane_id = (lax.broadcasted_iota(jnp.int32, (planes, LANES), 0) - HALO).astype(F32)
    south_end = jnp.where(has_s, 0, HALO).astype(F32)
    north_end = jnp.where(has_n, rows, rows - HALO).astype(F32)

    def masked(t, half):
        return jnp.where(jnp.abs(t) <= REACH, tap(t + half), 0.0)

    def split_blocks(home, size):
        block = jnp.floor(home * (1.0 / size))
        inner = home - block * size
        low = inner < size // 2
        return block, inner, jnp.where(low, block - 1.0, block + 1.0), jnp.where(low, -1.0 * size, 1.0 * size)

    def prepare(pk, brick, slot, at, width):
        for off in range(0, width, LANES):
            sl = pl.ds(pl.multiple_of(at + off, LANES), LANES)
            cz, cy, cx = [c.astype(F32) for c in split_cell(pk[4:5, sl].astype(jnp.int32), ny, nx)]
            hz, hy, hx = 0.5 - pk[5:6, sl], 0.5 - pk[6:7, sl], 0.5 - pk[7:8, sl]
            sum_z = jnp.sum(masked(iota8 - REACH, hz), axis=0, keepdims=True)
            wz_ref[slot, :, sl] = masked(plane_id - (cz + brick), hz) * (1.0 / sum_z)

            block, inner, beside, shift = split_blocks(cy + HALO, 8)
            t0 = iota8 - inner
            t1 = t0 + shift
            r0 = iota8 + block * 8
            r1 = iota8 + beside * 8
            v0 = jnp.where((r0 >= south_end) & (r0 < north_end), masked(t0, hy), 0.0)
            v1 = jnp.where((r1 >= south_end) & (r1 < north_end), masked(t1, hy), 0.0)
            scale = 1.0 / jnp.sum(v0 + v1, axis=0, keepdims=True)
            v0, v1 = v0 * scale, v1 * scale
            block, beside = jnp.broadcast_to(block, (8, LANES)), jnp.broadcast_to(beside, (8, LANES))
            for g in range(rows // 8):
                wy_ref[slot, 8 * g : 8 * g + 8, sl] = jnp.where(block == g, v0, jnp.where(beside == g, v1, 0.0))

            block, inner, beside, shift = split_blocks(cx, 16)
            t0 = iota16 - inner
            t1 = t0 + shift
            inside = (beside >= 0) & (beside < nx // 16)
            v0 = masked(t0, hx)
            v1 = jnp.where(inside, masked(t1, hx), 0.0)
            scale = 1.0 / jnp.sum(v0 + v1, axis=0, keepdims=True)
            v0, v1 = (v0 * scale).astype(jnp.bfloat16), (v1 * scale).astype(jnp.bfloat16)
            block = jnp.broadcast_to(block, (16, LANES)).astype(jnp.bfloat16)
            beside = jnp.broadcast_to(beside, (16, LANES)).astype(jnp.bfloat16)
            none = jnp.zeros((16, LANES), jnp.bfloat16)
            for g in range(nx // 16):
                wx_ref[slot, 16 * g : 16 * g + 16, sl] = jnp.where(block == g, v0, jnp.where(beside == g, v1, none))

    def deposit(pk, slot, lo, n, add, wide=1, after=None, parts=4):
        assert n % wide == 0

        def body(j, carry):
            i = lo + j * wide
            acc = None
            for at in range(0, slots, CHUNK):
                sl = pl.ds(at, CHUNK)
                wy = wy_ref[slot, :, sl]
                stack = []
                for h in range(wide):
                    scaled = pk[0:parts, sl] * wz_ref[slot, pl.ds(i + h, 1), sl]
                    stack += [scaled[k : k + 1] * wy for k in range(parts)]
                lhs = jnp.concatenate(stack, axis=0).astype(jnp.bfloat16)
                part = lax.dot_general(
                    lhs, wx_ref[slot, :, sl], (((1,), (1,)), ((), ())), preferred_element_type=F32
                )
                acc = part if acc is None else acc + part
            acc = acc.reshape(wide, parts, rows, nx)
            for h in range(wide):
                dep[i + h, 0:parts] = dep[i + h, 0:parts] + acc[h] if add else acc[h]
                if after is not None:
                    after(i + h)
            return carry

        lax.fori_loop(0, n // wide, body, 0)

    dep[0] = jnp.zeros((4, rows, nx), F32)
    dep[planes - 1] = jnp.zeros((4, rows, nx), F32)

    def prepare_all(pk, brick, slot):
        def body(i, carry):
            prepare(pk, brick, slot, i * 4 * LANES, 4 * LANES)
            return carry

        lax.fori_loop(0, slots // (4 * LANES), body, 0)

    prepare_all(pk_ref, 0.0, 0)
    reach = HALO + REACH
    side = (1 - 2 * odd).astype(F32) * nz
    lo_near, lo_far = (1 - odd) * (planes - reach), odd * (planes - reach)
    out_near, out_far = (1 - odd) * (planes - 1), odd * (planes - 1)
    reached = nz + 2 * REACH
    ahead = 4
    deposit(pk_ref, 0, HALO - REACH, ahead, False, OWN_WIDE)
    pl.semaphore_wait(barrier, count - 1)
    for c in near_copies:
        c.start()
    for c in loads[4:]:
        c.wait()
    start_y(den_y)
    start_y(p_y)
    deposit(pk_ref, 0, HALO - REACH + ahead, reached - ahead, False, OWN_WIDE)

    def tile_pair_of(i):
        return (
            remote(
                dep.at[i, :, pl.ds(ny, EDGE), :], tile_in.at[0, i], tile_send.at[i, 0], tile_recv.at[i, 0],
                {"gy": north_gy},
            ),
            remote(
                dep.at[i, :, pl.ds(0, EDGE), :], tile_in.at[1, i], tile_send.at[i, 1], tile_recv.at[i, 1],
                {"gy": south_gy},
            ),
        )

    def send_tiles(i):
        start_y(tile_pair_of(i))

    near_copies[0].wait()
    prepare_all(near.at[0], side, 1)
    for i in range(reach, planes - reach):
        send_tiles(i)
    deposit(near.at[0], 1, out_near, 1, True, 1, send_tiles, 2)
    deposit(near.at[0], 1, lo_near + odd, reach - 1, True, NEAR_WIDE, send_tiles)
    near_copies[1].wait()
    start_z(den_z)
    start_z(p_z)
    prepare_all(near.at[1], -side, 2)
    deposit(near.at[1], 2, out_far, 1, True, 1, send_tiles, 2)
    deposit(near.at[1], 2, lo_far + 1 - odd, reach - 1, True, NEAR_WIDE, send_tiles)

    def add_tiles(lo, n):
        def body(j, carry):
            i = lo + j
            wait_y(tile_pair_of(i))

            @pl.when(has_s)
            def _():
                dep[i, :, 0:EDGE, :] = dep[i, :, 0:EDGE, :] + tile_in[0, i]

            @pl.when(has_n)
            def _():
                dep[i, :, ny : ny + EDGE, :] = dep[i, :, ny : ny + EDGE, :] + tile_in[1, i]

            @pl.when(jnp.logical_not(has_s))
            def _():
                dep[i, :, HALO - 1 : HALO, :] = dep[i, :, HALO : HALO + 1, :]

            @pl.when(jnp.logical_not(has_n))
            def _():
                dep[i, :, HALO + ny : HALO + ny + 1, :] = dep[i, :, HALO + ny - 1 : HALO + ny, :]

            return carry

        lax.fori_loop(0, n, body, 0)

    def shifts_x(v, mirror=False):
        lane = lax.broadcasted_iota(jnp.int32, (v.shape[0], LANES), 1)
        parts = [v[:, at : at + LANES] for at in range(0, nx, LANES)]
        ups = [pltpu.roll(part, 1, 1) for part in parts]
        downs = [pltpu.roll(part, LANES - 1, 1) for part in parts]
        first_wall, last_wall = (parts[0], parts[-1]) if mirror else (0.0, 0.0)
        west = [jnp.where(lane == 0, ups[n - 1] if n else first_wall, u) for n, u in enumerate(ups)]
        east = [
            jnp.where(lane == LANES - 1, downs[n + 1] if n + 1 < len(parts) else last_wall, u)
            for n, u in enumerate(downs)
        ]
        return jnp.concatenate(west, axis=1), jnp.concatenate(east, axis=1)

    def sweep(src, dst, lo, n, last=False, ks=(0, 1, 2, 3)):
        sub = lax.broadcasted_iota(jnp.int32, (8, nx), 0)
        south_ghost = (sub == HALO - 1) & jnp.logical_not(has_s)
        north_ghost = (sub == (HALO + ny) % 8) & jnp.logical_not(has_n)

        def body(j, carry):
            i = lo + j
            for k in ks:

                def turned(t):
                    c = src[i, k, 8 * t : 8 * t + 8, :]
                    return c, pltpu.roll(c, 1, 0), pltpu.roll(c, 7, 0)

                lower, here = None, turned(0)
                for t in range(rows // 8):
                    upper = turned(t + 1) if t + 1 < rows // 8 else None
                    c, south, north = here
                    south = south if lower is None else jnp.where(sub == 0, lower[1], south)
                    north = north if upper is None else jnp.where(sub == 7, upper[2], north)
                    west, east = shifts_x(c, True)
                    at = slice(8 * t, 8 * t + 8)
                    beside = (src[i - 1, k, at, :] + src[i + 1, k, at, :]) + (south + north) + (west + east)
                    out = (1.0 - 6.0 * smooth_rate) * c + smooth_rate * beside
                    if t == 0:
                        out = jnp.where(south_ghost, 0.0 if last else pltpu.roll(out, 7, 0), out)
                    if upper is None:
                        out = jnp.where(north_ghost, 0.0 if last else pltpu.roll(out, 1, 0), out)
                    dst[i, k, at, :] = out
                    lower, here = here, upper
            return carry

        lax.fori_loop(0, n, body, 0)

    outer = (0, 1)
    half = planes // 2 - 2
    bufs = [dep, fld]
    add_tiles(lo_near + (odd - 1) * (planes - 2 * reach), planes - reach)
    sweep(dep, fld, odd + (1 - odd) * (planes - 2), 1, False, outer)
    sweep(dep, fld, 2 + (1 - odd) * half, half)
    add_tiles(lo_far, reach)
    sweep(dep, fld, 2 + odd * half, half)
    sweep(dep, fld, (1 - odd) + odd * (planes - 2), 1, False, outer)
    for s in range(1, SWEEPS - 1):
        for edge_plane in (s + 1, planes - s - 2):
            sweep(bufs[s % 2], bufs[(s + 1) % 2], edge_plane, 1, False, outer)
        sweep(bufs[s % 2], bufs[(s + 1) % 2], s + 2, planes - 2 * s - 4)
    before, f = bufs[(SWEEPS - 1) % 2], bufs[SWEEPS % 2]
    for edge_plane, inner_plane in ((HALO - 1, HALO), (HALO + nz, HALO + nz - 2)):
        sweep(before, f, edge_plane, 1, True, outer)
        sweep(before, f, inner_plane, 2, True)

    def own(v, shift=0):
        return pltpu.roll(v, rows - HALO - shift, 0)[0:ny]

    wait_y(den_y)
    wait_y(p_y)
    wait_z(den_z)
    wait_z(p_z)
    def mobility(z):
        g = own(1.0 / (1.0 + f[z + HALO, 0]))
        if 0 <= z < nz:
            gf_ref[z] = g
            for k in range(3):
                mom_ref[z, k] = own(f[z + HALO, k + 1])
            den = den_ref[z]
        else:
            den = halo_z[1, 0 if z < 0 else 1]
        mob[z + 1] = g / den

    own_row = lax.broadcasted_iota(jnp.int32, (ny, nx), 0)

    def shifts_y(v, south_row, north_row):
        south = jnp.where(own_row == 0, south_row, pltpu.roll(v, 1, 0))
        north = jnp.where(own_row == ny - 1, north_row, pltpu.roll(v, ny - 1, 0))
        return south, north

    def halo_rows(slot, z):
        if slot < 2:
            south, north = halo_y[slot, 0, z, 7:8, :], halo_y[slot, 1, z, 0:1, :]
        else:
            south, north = edge_in[slot - 2, 0, z : z + 1, :], edge_in[slot - 2, 1, z : z + 1, :]
        return jnp.where(has_s, south, 0.0), jnp.where(has_n, north, 0.0)

    def apply(v, slot, z):
        c = v[z]
        below = v[z - 1] if z > 0 else halo_z[slot, 0]
        above = v[z + 1] if z < nz - 1 else halo_z[slot, 1]
        south, north = shifts_y(c, *halo_rows(slot, z))
        west, east = shifts_x(c)
        coupled = (
            face_z[z] * below + face_z[z + 1] * above + face_s[z] * south + face_n[z] * north
            + face_w[z] * west + face_e[z] * east
        )
        return diag[z] * c - coupled

    def keep_edge(slot, z, v):
        edge[slot, 0, z : z + 1, :] = v[ny - 1 : ny]
        edge[slot, 1, z : z + 1, :] = v[0:1]

    def edge_pair(slot):
        return pair_y(
            slot, edge.at[slot - 2, 0], edge.at[slot - 2, 1], edge_in.at[slot - 2, 0], edge_in.at[slot - 2, 1]
        )

    inner_first = list(range(1, nz - 1)) + [0, nz - 1]
    z_z, w_z, z_y, w_y = pair_z(2, z_ref), pair_z(3, w_ref), edge_pair(2), edge_pair(3)
    def source(z):
        for side_z in (z, z + 1):
            face_z[side_z] = 0.5 * (mob[side_z] + mob[side_z + 1])
        m = mob[z + 1]
        gs = f[z + HALO, 0, HALO - 1 : HALO, :]
        gn = f[z + HALO, 0, HALO + ny : HALO + ny + 1, :]
        ms = jnp.where(has_s, 1.0 / (1.0 + gs) / halo_y[1, 0, z, 7:8, :], 0.0)
        mn = jnp.where(has_n, 1.0 / (1.0 + gn) / halo_y[1, 1, z, 0:1, :], 0.0)
        south, north = shifts_y(m, ms, mn)
        west, east = shifts_x(m)
        fs, fn, fw, fe = 0.5 * (m + south), 0.5 * (m + north), 0.5 * (m + west), 0.5 * (m + east)
        face_s[z], face_n[z], face_w[z], face_e[z] = fs, fn, fw, fe
        dg = stiffness * m + face_z[z] + face_z[z + 1] + fs + fn + fw + fe
        diag[z] = dg
        mz_d, mz_u = own(f[z + HALO - 1, 1]), own(f[z + HALO + 1, 1])
        my = f[z + HALO, 2]
        xw, xe = shifts_x(own(f[z + HALO, 3]))
        spread = 0.5 * (mz_u - mz_d) + 0.5 * (own(my, 1) - own(my, -1)) + 0.5 * (xe - xw)
        r0 = div_ref[z] - spread - apply(p_ref, 0, z)
        r_ref[z] = r0
        z0 = r0 / dg
        z_ref[z] = z0
        keep_edge(0, z, z0)

    for z in (-1, 0, 1, nz - 2, nz - 1, nz):
        mobility(z)
    for z in (0, nz - 1):
        source(z)
    start_z(z_z)
    sweep(before, f, HALO + 2, nz - 4, True)
    for z in range(2, nz - 2):
        mobility(z)
    for z in range(1, nz - 1):
        source(z)
    start_y(z_y)

    def fold(v):
        part = jnp.sum(v, axis=0, keepdims=True)
        out = part[:, 0:LANES]
        for at in range(LANES, nx, LANES):
            out = out + part[:, at : at + LANES]
        for step in (64, 32):
            out = out + pltpu.roll(out, step, 1)
        return out

    sums = [jnp.zeros((ny, nx), F32)] * 4
    wait_y(z_y)
    for z in inner_first:
        if z == 0:
            wait_z(z_z)
        q = apply(z_ref, 2, z)
        w = q / diag[z]
        q_ref[z] = q
        w_ref[z] = w
        keep_edge(1, z, w)
    start_z(w_z)
    start_y(w_y)
    for z in range(nz):
        sums[0] = sums[0] + r_ref[z] * z_ref[z]
        sums[1] = sums[1] + z_ref[z] * q_ref[z]
        sums[2] = sums[2] + q_ref[z] * w_ref[z]
    wait_y(w_y)
    for z in inner_first:
        if z == 0:
            wait_z(w_z)
        aw = apply(w_ref, 3, z)
        aw_ref[z] = aw
        sums[3] = sums[3] + w_ref[z] * aw
    quarter = lax.broadcasted_iota(jnp.int32, (1, LANES), 1) // 32
    line = fold(sums[3])
    for n in range(3):
        line = jnp.where(quarter == n, fold(sums[n]), line)
    row_ref[0] = line

    def row_copy(d):
        return remote(row_ref.at[0], red.at[me], row_send.at[d - 1], row_recv.at[me], place_of(d))

    def row_from(d):
        whom = lax.rem(me + count - d, count)
        return remote(row_ref.at[0], red.at[whom], row_send.at[d - 1], row_recv.at[whom], place_of(d))

    each_other(lambda d: row_copy(d).start())
    red[me] = line
    each_other(lambda d: row_copy(d).wait_send())
    each_other(lambda d: row_from(d).wait_recv())
    total = jnp.sum(red[...], axis=0)
    norm0, curve0, mix, square = [
        jnp.sum(jnp.where(quarter == n, total, 0.0), axis=1, keepdims=True) for n in range(4)
    ]
    step0 = norm0 / curve0
    norm1 = norm0 - 2.0 * step0 * curve0 + step0 * step0 * mix
    curve1 = curve0 - 2.0 * step0 * mix + step0 * step0 * square
    beta = norm1 / norm0
    step1 = norm1 / (curve1 - beta * norm1 / step0)
    along, back = step0 + step1 * (1.0 + beta), step0 * step1
    for z in range(nz):
        out_ref[z] = p_ref[z] + along * z_ref[z] - back * w_ref[z]
        res_ref[z] = r_ref[z] - along * q_ref[z] + back * aw_ref[z]


def pass_kernel(*refs):
    ins, outs, put = refs[0:4], refs[4:8], refs[8]
    ways = [pltpu.make_async_copy(ins[n], outs[n], put.at[n]) for n in range(4)]
    for c in ways:
        c.start()
    for c in ways:
        c.wait()


def on_device(ngz, ngy, parcel_cell, parcel_offset, parcel_volume, parcel_force, brick_counts,
              divergence, pressure_prev, gas_density):
    nz, ny, nx = divergence.shape
    slots = parcel_cell.shape[0]
    planes, rows = nz + 2 * HALO, ny + EDGE
    field = jax.ShapeDtypeStruct((nz, ny, nx), F32)
    own = pltpu.VMEM((nz, ny, nx), F32)
    dma = pltpu.SemaphoreType.DMA
    vmem = pl.BlockSpec(memory_space=pltpu.VMEM)
    hbm = pl.BlockSpec(memory_space=pl.ANY)
    shapes = (field, jax.ShapeDtypeStruct((nz, 3, ny, nx), F32), field, field)
    count = ngz * ngy
    made = pl.pallas_call(
        functools.partial(step_kernel, ngz, ngy, nz, ny, nx, slots),
        out_shape=tuple(pltpu.VMEM(shape.shape, F32) for shape in shapes),
        in_specs=[pl.BlockSpec(memory_space=pltpu.SMEM)] + [hbm] * 7,
        out_specs=(vmem,) * 4,
        scratch_shapes=[
            pltpu.VMEM((1, slots), jnp.int32), pltpu.VMEM((3, slots), F32),
            pltpu.VMEM((1, slots), F32), pltpu.VMEM((3, slots), F32),
            own, own, own,
            pltpu.VMEM((8, slots), F32),
            pltpu.VMEM((2, 8, slots), F32),
            pltpu.VMEM((3, planes, slots), F32),
            pltpu.VMEM((3, rows, slots), F32),
            pltpu.VMEM((3, nx, slots), jnp.bfloat16),
            pltpu.VMEM((planes, 4, rows, nx), F32),
            pltpu.VMEM((planes, 4, rows, nx), F32),
            pltpu.VMEM((2, planes, 4, EDGE, nx), F32),
            pltpu.VMEM((4, 2, ny, nx), F32),
            pltpu.VMEM((2, 2, nz, 8, nx), F32),
            pltpu.VMEM((2, 2, nz, nx), F32),
            pltpu.VMEM((2, 2, nz, nx), F32),
            pltpu.VMEM((nz + 2, ny, nx), F32),
            pltpu.VMEM((nz + 1, ny, nx), F32),
            own, own, own, own, own,
            own, own, own, own, own,
            pltpu.VMEM((1, 1, 128), F32),
            pltpu.VMEM((count, 1, 128), F32),
            dma((7,)), dma((2,)), dma((2,)),
            dma((planes, 2)), dma((planes, 2)),
            dma((4, 2)), dma((4, 2)), dma((4, 2)), dma((4, 2)),
            dma((count,)), dma((count,)),
        ],
        compiler_params=pltpu.CompilerParams(
            collective_id=0, has_side_effects=True, vmem_limit_bytes=48 * 1024 * 1024
        ),
    )(brick_counts, *[
        pltpu.with_memory_space_constraint(array, pltpu.HBM)
        for array in (
            parcel_cell[None, :], parcel_offset, parcel_volume[None, :], parcel_force,
            divergence, pressure_prev, gas_density,
        )
    ])
    return pl.pallas_call(
        pass_kernel,
        out_shape=shapes,
        in_specs=[vmem] * 4,
        out_specs=(hbm,) * 4,
        scratch_shapes=[dma((4,))],
    )(*[pltpu.with_memory_space_constraint(array, pltpu.VMEM) for array in made])


def solution(mesh):
    ngz, ngy = mesh.shape["gz"], mesh.shape["gy"]
    return jax.shard_map(
        functools.partial(on_device, ngz, ngy),
        mesh=mesh,
        in_specs=(
            P(("gz", "gy")),
            P(None, ("gz", "gy")),
            P(("gz", "gy")),
            P(None, ("gz", "gy")),
            P("gz", "gy"),
            P("gz", "gy", None),
            P("gz", "gy", None),
            P("gz", "gy", None),
        ),
        out_specs=(
            P("gz", "gy", None),
            P("gz", None, "gy", None),
            P("gz", "gy", None),
            P("gz", "gy", None),
        ),
        check_vma=False,
    )
```
